512 devices in a mesh: seq: 64 (over z, x, y_hi), ch: 8 (over y_lo, core).
Axes of the slice: x: 4, y: 8 (y_hi: 2, y_lo: 4; y = y_hi * 4 + y_lo), z: 8, core: 2. Of those that a mesh axis runs over, the one named last changes fastest.
Arguments:
- queries: bfloat16 [4096, 8192], P('ch', 'seq'), may hold values from -6 to 6
- key_feat: bfloat16 [4096, 8192], P('ch', 'seq'), may hold values from -6 to 6
- value_feat: bfloat16 [4096, 8192], P('ch', 'seq'), may hold values from -6 to 6
- out_grad: bfloat16 [4096, 8192], P('ch', 'seq'), may hold values from -6 to 6
- out_weight: bfloat16 [4096, 4096], P('ch', 'seq'), may hold values from -0.09375 to 0.09375
- long_filter: bfloat16 [4096, 8192], P('ch', 'seq'), may hold values from -0.125 to 0.125
- short_filter: bfloat16 [256, 128], P('ch'), may hold values from -0.5 to 0.5
Outputs:
- d_key: bfloat16 [4096, 8192], P('ch', 'seq')
- d_value: bfloat16 [4096, 8192], P('ch', 'seq')
- d_filter: float32 [256, 128], P('ch')
The draws below stay inside these ranges and needn't reach their ends.
All inputs are finite; a program needn't handle non-finite values.
Results may differ from the reference program's by a relative error of at most 0.0064.
Values may be sent and summed in bfloat16 or wider, within the bound.
No kernel may reach another device: no remote copies, remote signals or barrier semaphores. Data moves between devices by JAX's collectives and lax.ppermute only.
A program may use at most 64 MiB of HBM per device.

```python
import jax
import jax.numpy as jnp
from jax import lax

D = 4096
G = 256
TAPS = 128
SEQ = 8192


def levels(own_key, shape, cuts, low, top_value):
    def one(axis_at, shards_of):
        heights = jax.random.uniform(jax.random.fold_in(jax.random.fold_in(own_key, 6), axis_at), (shards_of,), jnp.float32, low / len(cuts), top_value / len(cuts))
        return jnp.repeat(jnp.exp(heights), shape[axis_at] // shards_of).reshape((-1,) + (1,) * (len(shape) - axis_at - 1))

    loudness = one(*cuts[0])
    for cut in cuts[1:]:
        loudness = loudness * one(*cut)
    return loudness


def gaussian(rng, extent, width, reach, pieces=(), kind=jnp.bfloat16):
    values = width * jax.random.normal(rng, extent, jnp.float32)
    if pieces:
        values = values * levels(rng, extent, pieces, -0.22, 0.18)
    return jnp.clip(values, -reach, reach).astype(kind)


def setup_inputs(seed: int = 0) -> dict:
    streams_of = jax.random.split(jax.random.key(seed), 8)
    return {
        "queries": gaussian(streams_of[0], (D, SEQ), 1.0, 6.0, ((0, 8), (1, 64))),
        "key_feat": gaussian(streams_of[1], (D, SEQ), 1.0, 6.0, ((0, 8), (1, 64))),
        "value_feat": gaussian(streams_of[2], (D, SEQ), 1.0, 6.0, ((0, 8), (1, 64))),
        "out_grad": gaussian(streams_of[3], (D, SEQ), 1.0, 6.0, ((0, 8), (1, 64))),
        "out_weight": gaussian(streams_of[4], (D, D), D ** -0.5, 0.09375, ((0, 8), (1, 64))),
        "long_filter": gaussian(streams_of[5], (D, SEQ), (SEQ // 4) ** -0.5, 0.125, ((0, 8), (1, 64))),
        "short_filter": gaussian(streams_of[6], (G, TAPS), TAPS ** -0.5, 0.5, ((0, 8),)),
    }


def long_adjoint(pair):
    grads, filters = pair
    length = 2 * grads.shape[1]
    spectrum_g = jnp.fft.rfft(grads.astype(jnp.float32), n=length, axis=1)
    spectrum_h = jnp.fft.rfft(filters.astype(jnp.float32), n=length, axis=1)
    back = jnp.fft.irfft(jnp.conj(spectrum_h) * spectrum_g, n=length, axis=1)
    return back[:, :grads.shape[1]].astype(jnp.float32)

def reference(queries, key_feat, value_feat, out_grad, out_weight, long_filter, short_filter):
    d_z = jnp.dot(out_weight, out_grad, preferred_element_type=jnp.float32)
    d_c = (d_z * queries.astype(jnp.float32)).astype(jnp.bfloat16)
    block = 256
    blocks = D // block
    d_w = lax.map(long_adjoint, (d_c.reshape(blocks, block, SEQ), long_filter.reshape(blocks, block, SEQ)))
    d_w = d_w.reshape(D, SEQ).astype(jnp.bfloat16)
    per_chan = jnp.repeat(short_filter.astype(jnp.float32), D // G, axis=0)
    values = value_feat.astype(jnp.float32)
    padded_v = jnp.pad(values, ((0, 0), (TAPS - 1, 0)))

    def shifted_back(offset):
        start = (jnp.int32(TAPS - 1) - offset).astype(jnp.int32)
        return lax.dynamic_slice_in_dim(padded_v, start, SEQ, 1)

    def tap_column(offset):
        return lax.dynamic_slice_in_dim(per_chan, offset.astype(jnp.int32), 1, 1)

    def add_filtered(offset, acc):
        return acc + tap_column(offset) * shifted_back(offset)
    filtered = lax.fori_loop(jnp.int32(0), jnp.int32(TAPS), add_filtered, jnp.zeros((D, SEQ), jnp.float32))
    d_key = (d_w.astype(jnp.float32) * filtered).astype(jnp.bfloat16)
    d_vf = (d_w.astype(jnp.float32) * key_feat.astype(jnp.float32)).astype(jnp.bfloat16)
    grads = d_vf.astype(jnp.float32)
    padded_g = jnp.pad(grads, ((0, 0), (0, TAPS - 1)))

    def add_value(offset, acc):
        ahead = lax.dynamic_slice_in_dim(padded_g, offset.astype(jnp.int32), SEQ, 1)
        return acc + tap_column(offset) * ahead
    d_value = lax.fori_loop(jnp.int32(0), jnp.int32(TAPS), add_value, jnp.zeros((D, SEQ), jnp.float32))
    d_value = d_value.astype(jnp.bfloat16)

    def tap_grad(offset):
        per_channel = lax.optimization_barrier(jnp.sum(grads * shifted_back(offset), axis=1))
        return per_channel.reshape(G, D // G).sum(axis=1)
    offsets = jnp.arange(TAPS, dtype=jnp.int32)
    grouped = lax.map(tap_grad, offsets)
    d_filter = jnp.transpose(grouped) / jnp.sqrt(jnp.float32(SEQ * (D // G)))
    return (d_key, d_value, d_filter)
```

```python
import math

import jax
import jax.numpy as jnp
from jax import lax
from jax.sharding import Mesh, PartitionSpec as P

highest = lax.Precision.HIGHEST
SEQ = ("z", "x", "yh")
CH = ("yl", "core")
SPLIT = {"z": 8, "x": 4, "yh": 2, "yl": 4, "core": 2}


def swap(value, axes):
    return lax.all_to_all(value, axes, split_axis=0, concat_axis=0, tiled=True)


def angle_table(first, second, modulus):
    left = lax.broadcasted_iota(jnp.int32, (first, second), 0)
    right = lax.broadcasted_iota(jnp.int32, (first, second), 1)
    phase = (left * right % modulus).astype(jnp.float32) * (2.0 * math.pi / modulus)
    return (jnp.cos(phase), jnp.sin(phase))


def contract(form, first, second):
    return jnp.einsum(form, first, second, precision=highest)


def spectral(grads, filters):
    half, items, inner = grads.shape
    outer = 2 * half
    total_len = outer * inner
    cos_p, sin_p = angle_table(outer, half, outer)
    cos_t, sin_t = angle_table(outer, inner, total_len)
    cos_q, sin_q = angle_table(inner, inner, inner)

    def forward(series):
        series = series.astype(jnp.float32)
        first_re = contract("kn,ncq->ckq", cos_p, series)
        first_im = -contract("kn,ncq->ckq", sin_p, series)
        turned_re = first_re * cos_t + first_im * sin_t
        turned_im = first_im * cos_t - first_re * sin_t
        spec_re = contract("ckq,qm->ckm", turned_re, cos_q) + contract(
            "ckq,qm->ckm", turned_im, sin_q
        )
        spec_im = contract("ckq,qm->ckm", turned_im, cos_q) - contract(
            "ckq,qm->ckm", turned_re, sin_q
        )
        return (spec_re, spec_im)

    grad_re, grad_im = forward(grads)
    filt_re, filt_im = forward(filters)
    prod_re = filt_re * grad_re + filt_im * grad_im
    prod_im = filt_re * grad_im - filt_im * grad_re
    back_re = contract("ckq,qm->ckm", prod_re, cos_q) - contract("ckq,qm->ckm", prod_im, sin_q)
    back_im = contract("ckq,qm->ckm", prod_im, cos_q) + contract("ckq,qm->ckm", prod_re, sin_q)
    twist_re = back_re * cos_t - back_im * sin_t
    twist_im = back_im * cos_t + back_re * sin_t
    result = contract("kn,ckq->ncq", cos_p, twist_re) - contract("kn,ckq->ncq", sin_p, twist_im)
    return result / total_len


def local(queries, key_feat, value_feat, out_grad, out_weight, long_filter, short_filter):
    channels, row_count = out_grad.shape
    group_count, tap_count = short_filter.shape
    per_group = channels // group_count
    split = SPLIT["x"] * SPLIT["yh"]
    seq_devices = SPLIT["z"] * split
    items = channels // seq_devices
    features = out_weight.shape[1]

    pieces = [
        a.reshape(seq_devices, items, row_count)
        for a in (long_filter, key_feat, value_feat, queries)
    ]
    moved = swap(jnp.concatenate(pieces, axis=1), SEQ)
    filters, keys, values, gates = jnp.split(moved, 4, axis=1)

    weight = jnp.broadcast_to(out_weight.T[None], (SPLIT["z"], features, channels))
    weight = swap(weight, ("z",))
    weight = weight.reshape(SPLIT["yl"], SPLIT["core"], features, channels)
    grad = out_grad.reshape(split, 1, features, row_count)
    grad = jnp.broadcast_to(grad, (split, SPLIT["yl"], features, row_count))
    grad = swap(grad.reshape(split * SPLIT["yl"], features, row_count), ("x", "yh", "yl"))
    grad = jnp.broadcast_to(grad[None], (SPLIT["core"],) + grad.shape)
    grad = swap(grad, ("core",))
    grad = grad.reshape(SPLIT["core"], split, SPLIT["yl"], features, row_count)
    partial = jnp.einsum(
        "ycoi,csyot->sit", weight, grad, preferred_element_type=jnp.float32
    ).astype(jnp.bfloat16)
    partial = partial.reshape(split, seq_devices, items, row_count).transpose(1, 0, 2, 3)
    partial = swap(partial, SEQ)
    partial = partial.reshape(SPLIT["z"], split, split, items, row_count)
    d_z = jnp.sum(partial.astype(jnp.float32), axis=1).reshape(seq_devices, items, row_count)
    d_c = (d_z * gates.astype(jnp.float32)).astype(jnp.bfloat16)

    d_w = spectral(d_c, filters).astype(jnp.bfloat16).astype(jnp.float32)
    place = lax.axis_index(SEQ) * items // per_group
    taps = lax.dynamic_slice_in_dim(short_filter, place, 1, 0)
    lag = lax.broadcasted_iota(jnp.int32, (tap_count, 2 * tap_count), 1) - lax.broadcasted_iota(
        jnp.int32, (tap_count, 2 * tap_count), 0
    )
    padded = jnp.pad(taps[0], (0, tap_count + 1))
    toeplitz = jnp.tile(padded, tap_count)[: 2 * tap_count * tap_count]
    toeplitz = toeplitz.reshape(tap_count, 2 * tap_count)
    zero = jnp.zeros((1, items, row_count), jnp.bfloat16)
    value_win = jnp.concatenate(
        [jnp.concatenate([zero, values[:-1]], axis=0), values], axis=2
    )
    filtered = jnp.einsum(
        "tw,bcw->bct", toeplitz[::-1, ::-1], value_win, preferred_element_type=jnp.float32
    )
    d_key = (d_w * filtered).astype(jnp.bfloat16)
    d_vf = (d_w * keys.astype(jnp.float32)).astype(jnp.bfloat16)
    grad_win = jnp.concatenate(
        [d_vf, jnp.concatenate([d_vf[1:], zero], axis=0)], axis=2
    )
    d_value = jnp.einsum(
        "tw,bcw->bct", toeplitz, grad_win, preferred_element_type=jnp.float32
    ).astype(jnp.bfloat16)
    corr = jnp.einsum("bct,bcw->tw", d_vf, value_win, preferred_element_type=jnp.float32)
    flat = jnp.pad(corr.reshape(-1), (0, tap_count))
    skewed = flat.reshape(tap_count, 2 * tap_count + 1)
    part = jnp.sum(skewed, axis=0)[1 : tap_count + 1][::-1]
    scale_factor = 1.0 / math.sqrt(row_count * seq_devices * per_group)
    part = part * scale_factor
    high = part.astype(jnp.bfloat16)
    low = (part - high.astype(jnp.float32)).astype(jnp.bfloat16)
    both = jnp.concatenate([high[None], low[None], jnp.zeros((items - 2, tap_count), jnp.bfloat16)])
    both = jnp.broadcast_to(both[None], (seq_devices, items, tap_count))
    home = swap(jnp.concatenate([d_key, d_value, both], axis=1), SEQ)
    d_key, d_value, both = jnp.split(home, 3, axis=1)
    both = both[:, 0].astype(jnp.float32) + both[:, 1].astype(jnp.float32)
    d_filter = jnp.sum(both.reshape(group_count, seq_devices // group_count, tap_count), axis=1)
    return (d_key.reshape(channels, row_count), d_value.reshape(channels, row_count), d_filter)


def solution(mesh):
    fine = Mesh(mesh.devices.reshape(tuple(SPLIT.values())), tuple(SPLIT))
    placed = (P(CH, SEQ),) * 6 + (P(CH, None),)
    return jax.shard_map(
        local,
        mesh=fine,
        in_specs=placed,
        out_specs=(P(CH, SEQ), P(CH, SEQ), P(CH, None)),
        check_vma=False,
    )
```

```python
import math

import jax
import jax.numpy as jnp
import numpy as np
from jax import lax
from jax.experimental import pallas as pl
from jax.experimental.pallas import tpu as pltpu
from jax.sharding import Mesh, PartitionSpec as P


SEQ = ("z", "x", "yh")
CH = ("yl", "core")
SPLIT = {"z": 8, "x": 4, "yh": 2, "yl": 4, "core": 2}
PARTS = ("x", "yh")
SHIFTS = (0, 1, 2, -1)
VMEM = pl.BlockSpec(memory_space=pltpu.VMEM)
INNER = 128
HALF = 64
LINES = 80


def swap(value, axes):
    return lax.all_to_all(value, axes, split_axis=0, concat_axis=0, tiled=True)


def flip(value, axis, bit):
    count = SPLIT[axis]
    return lax.ppermute(value, axis, [(i, i ^ bit) for i in range(count)])


def high_low(table):
    high = table.astype(jnp.bfloat16)
    low = (table - high.astype(np.float64)).astype(jnp.bfloat16)
    return high, low


def spectral_tables():
    total = 2 * HALF * INNER
    lines = np.arange(LINES)[:, None]
    kept = (lines <= HALF).astype(np.float64)
    weight = np.where((lines == 0) | (lines == HALF), 1.0, 2.0) * kept / total
    blocks = np.arange(HALF)[None, :]
    turn = 2.0 * math.pi * (lines * blocks % (2 * HALF)) / (2 * HALF)
    first = np.concatenate([np.cos(turn) * kept, -np.sin(turn) * kept])
    last = np.concatenate([np.cos(turn) * weight, -np.sin(turn) * weight]).T
    place = np.arange(INNER)
    twist = 2.0 * math.pi * (lines * place[None, :] % total) / total
    inner = 2.0 * math.pi * (place[:, None] * place[None, :] % INNER) / INNER
    cos_q, sin_q = np.cos(inner), np.sin(inner)
    middle = np.block([[cos_q, -sin_q], [sin_q, cos_q]])
    first_high, first_low = high_low(first)
    last_high, last_low = high_low(last)
    middle_high, middle_low = high_low(middle)
    return (
        np.concatenate([first_high, first_low], axis=1),
        np.concatenate([last_high, last_high, last_low], axis=1),
        middle_high,
        middle_low,
        np.cos(twist).astype(np.float32),
        np.sin(twist).astype(np.float32),
    )


def dot(first, second, first_dim=1, second_dim=0):
    return lax.dot_general(
        first,
        second,
        (((first_dim,), (second_dim,)), ((), ())),
        preferred_element_type=jnp.float32,
    )


def two_parts(value):
    high = value.astype(jnp.bfloat16)
    return high, (value - high.astype(jnp.float32)).astype(jnp.bfloat16)


def product(value, table_high, table_low, table_dim):
    high, low = two_parts(value)
    return (
        dot(high, table_high, 1, table_dim)
        + dot(high, table_low, 1, table_dim)
        + dot(low, table_high, 1, table_dim)
    )


def spectrum(rows_ref, items, first, middle_high, middle_low, cos_t, sin_t):
    series = jnp.concatenate(
        [rows_ref[pl.ds(c, HALF, stride=items), :] for c in range(items)], axis=1
    ).astype(jnp.bfloat16)
    lines = dot(first, jnp.concatenate([series, series], axis=0))
    turned = []
    for c in range(items):
        at = slice(c * INNER, (c + 1) * INNER)
        real, imag = lines[:LINES, at], lines[LINES:, at]
        turned.append(
            jnp.concatenate([real * cos_t + imag * sin_t, imag * cos_t - real * sin_t], axis=1)
        )
    return product(jnp.concatenate(turned, axis=0), middle_high, middle_low, 0)


def conv_kernel(
    scale,
    near,
    home_ref,
    taps_ref,
    back_taps_ref,
    first_ref,
    last_ref,
    high_ref,
    low_ref,
    cos_ref,
    sin_ref,
    out_ref,
    rows_ref,
    back_ref,
):
    count, inner = rows_ref.shape
    items = count // HALF
    parts = home_ref.shape[1] - 4
    first = first_ref[...]
    cos_t, sin_t = cos_ref[...], sin_ref[...]
    high, low = high_ref[...], low_ref[...]
    rows_ref[...] = home_ref[:, parts].astype(jnp.float32).reshape(count, inner)
    filt = spectrum(rows_ref, items, first, high, low, cos_t, sin_t)
    filt_re, filt_im = filt[:, :inner], filt[:, inner:]
    values = home_ref[:, parts + 2].astype(jnp.float32).reshape(count, inner)
    values = values.astype(jnp.bfloat16)
    before = dot(values, back_taps_ref[:, :inner], 1, 1)
    filtered = dot(values, back_taps_ref[:, inner:], 1, 1)
    filtered += jnp.concatenate([jnp.zeros((items, inner), jnp.float32), before[:-items]], axis=0)
    for block in range(HALF):
        far, rest = divmod(block, parts * near)
        shard, side = divmod(rest, near)
        total = home_ref[far * parts * near + side, shard].astype(jnp.float32)
        for p in range(1, parts):
            total += home_ref[(far * parts + p) * near + side, shard].astype(jnp.float32)
        gate = home_ref[block, parts + 3].astype(jnp.float32)
        total = (total * gate).astype(jnp.bfloat16)
        rows_ref[block * items : (block + 1) * items, :] = total.astype(jnp.float32)
    grad = spectrum(rows_ref, items, first, high, low, cos_t, sin_t)
    grad_re, grad_im = grad[:, :inner], grad[:, inner:]
    both = jnp.concatenate(
        [filt_re * grad_re + filt_im * grad_im, filt_re * grad_im - filt_im * grad_re], axis=1
    )
    both = product(both, high, low, 1)
    lines = []
    for c in range(items):
        at = slice(c * LINES, (c + 1) * LINES)
        real, imag = both[at, :inner], both[at, inner:]
        lines.append(
            jnp.concatenate([real * cos_t - imag * sin_t, imag * cos_t + real * sin_t], axis=0)
        )
    line_high, line_low = two_parts(jnp.concatenate(lines, axis=1))
    result = dot(last_ref[...], jnp.concatenate([line_high, line_low, line_high], axis=0))
    for c in range(items):
        back_ref[pl.ds(c, HALF, stride=items), :] = result[:, c * inner : (c + 1) * inner]
    d_w = back_ref[...].astype(jnp.bfloat16).astype(jnp.float32)
    d_key = d_w * filtered
    keys = home_ref[:, parts + 1].astype(jnp.float32).reshape(count, inner)
    d_vf = (d_w * keys).astype(jnp.bfloat16).astype(jnp.float32)
    ahead = jnp.concatenate([d_vf[items:], jnp.zeros((items, inner), jnp.float32)], axis=0)
    pair = jnp.concatenate([d_vf, ahead], axis=1).astype(jnp.bfloat16)
    d_value = dot(pair, taps_ref[...], 1, 1)
    corr = dot(pair, values, 0, 0)
    corr = jnp.concatenate([corr[inner:], corr[:inner]], axis=1)
    row = lax.broadcasted_iota(jnp.int32, corr.shape, 0)
    shift = 1
    while shift < inner:
        moved = pltpu.roll(corr, 2 * inner - shift, 1)
        corr = jnp.where((row & shift) != 0, moved, corr)
        shift *= 2
    sums = jnp.sum(corr, axis=0, keepdims=True) * scale
    sums = pltpu.roll(jnp.broadcast_to(sums, (16, 2 * inner)), 2 * inner - 1, 1)[:, :inner]
    sum_high = sums.astype(jnp.bfloat16).astype(jnp.float32)
    line = lax.broadcasted_iota(jnp.int32, sums.shape, 0)
    sums = jnp.where(line == 0, sum_high, jnp.where(line == 1, sums - sum_high, 0.0))
    across = lax.broadcasted_iota(jnp.int32, (inner, inner), 0)
    across = across + lax.broadcasted_iota(jnp.int32, (inner, inner), 1)
    mirror = jnp.where(across == inner - 1, 1.0, 0.0).astype(jnp.bfloat16)
    sums = dot(sums.astype(jnp.bfloat16), mirror)[:items]
    out_ref[:, 0:items, :] = d_key.reshape(HALF, items, inner).astype(jnp.bfloat16)
    out_ref[:, items : 2 * items, :] = d_value.reshape(HALF, items, inner).astype(jnp.bfloat16)
    out_ref[:, 2 * items :, :] = jnp.broadcast_to(sums[None], (HALF, items, inner)).astype(
        jnp.bfloat16
    )


def project_kernel(mine_ref, other_ref, *rest):
    block_refs, own_refs, (out_ref, held_ref) = rest[:4], rest[4:-2], rest[-2:]
    shards, lines, depth, rows = mine_ref.shape
    z, core = lax.axis_index("z"), lax.axis_index("core")
    for shift, block_ref in zip(SHIFTS, block_refs):
        for e in range(2):
            source = ((z - shift) & 7) ^ (4 * e)
            place = (source & 6) + ((source & 1) ^ core)
            at = pl.multiple_of(place * depth, depth)
            held_ref[pl.ds(at, depth), :] = block_ref[e]
    weight = held_ref[...].T
    dests = out_ref.shape[0]
    for i, own_ref in enumerate(own_refs):
        out_ref[:, shards + i] = own_ref[...]
    for s in range(0, shards, 2):
        columns = []
        for t in (s, s + 1):
            stack = []
            for y in range(lines):
                stack += [mine_ref[t, y], other_ref[t, y]]
            columns.append(jnp.concatenate(stack, axis=0))
        result = dot(weight, jnp.concatenate(columns, axis=1))
        for i, t in enumerate((s, s + 1)):
            piece = result[:, i * rows : (i + 1) * rows]
            out_ref[:, t] = piece.reshape(dests, -1, rows).astype(jnp.bfloat16)


def local(queries, key_feat, value_feat, out_grad, out_weight, long_filter, short_filter):
    channels, row_count = out_grad.shape
    group_count, tap_count = short_filter.shape
    per_group = channels // group_count
    split = math.prod(SPLIT[a] for a in PARTS)
    seq_devices = SPLIT["z"] * SPLIT["x"] * SPLIT["yh"]
    items = channels // seq_devices
    depth = channels // split

    count_z = SPLIT["z"]
    weight = out_weight.T
    opposite = flip(weight, "z", 4)
    blocks = [jnp.stack([weight, opposite])]
    for k in SHIFTS[1:]:
        ring = [(i, (i + k) % count_z) for i in range(count_z)]
        blocks.append(lax.ppermute(blocks[0], "z", ring))

    grad = out_grad.reshape(split, 1, depth, row_count)
    grad = jnp.broadcast_to(grad, (split, SPLIT["yl"], depth, row_count))
    grad = swap(grad.reshape(split * SPLIT["yl"], depth, row_count), PARTS + ("yl",))
    other = flip(grad, "core", 1)
    form = (split, SPLIT["yl"], depth, row_count)

    pieces = [
        a.reshape(seq_devices, items, row_count)
        for a in (long_filter, key_feat, value_feat, queries)
    ]
    partial = pl.pallas_call(
        project_kernel,
        out_shape=jax.ShapeDtypeStruct((seq_devices, split + 4, items, row_count), jnp.bfloat16),
        in_specs=[VMEM] * 10,
        out_specs=VMEM,
        scratch_shapes=[pltpu.VMEM((8 * depth, channels), jnp.bfloat16)],
        cost_estimate=pl.CostEstimate(
            flops=2 * channels * 8 * depth * split * row_count, bytes_accessed=3 << 20, transcendentals=0
        ),
        compiler_params=pltpu.CompilerParams(vmem_limit_bytes=24 << 20),
        name="project",
    )(grad.reshape(form), other.reshape(form), *blocks, *pieces)
    partial = swap(partial, SEQ)
    near = seq_devices // (SPLIT["z"] * split)
    near = seq_devices // (SPLIT["z"] * split)

    place = lax.axis_index(SEQ) * items // per_group
    taps = lax.dynamic_slice_in_dim(short_filter, place, 1, 0)
    padded = jnp.pad(taps[0], (0, tap_count + 1))
    toeplitz = jnp.tile(padded, tap_count)[: 2 * tap_count * tap_count]
    toeplitz = toeplitz.reshape(tap_count, 2 * tap_count)
    first, last, high, low, cos_t, sin_t = spectral_tables()
    count = seq_devices * items
    scale = 1.0 / math.sqrt(row_count * seq_devices * per_group)

    def conv(*refs):
        conv_kernel(scale, near, *refs)

    home = pl.pallas_call(
        conv,
        out_shape=jax.ShapeDtypeStruct((seq_devices, 3 * items, row_count), jnp.bfloat16),
        in_specs=[VMEM] * 9,
        out_specs=VMEM,
        scratch_shapes=[pltpu.VMEM((count, row_count), jnp.float32)] * 2,
        cost_estimate=pl.CostEstimate(flops=1 << 31, bytes_accessed=4 << 20, transcendentals=0),
        compiler_params=pltpu.CompilerParams(vmem_limit_bytes=24 << 20),
        name="conv",
    )(partial, toeplitz, toeplitz[::-1, ::-1], first, last, high, low, cos_t, sin_t)
    home = home.reshape(seq_devices, 3 * items // 2, 2, row_count)[:, : items + 1]
    home = swap(home, SEQ)
    d_key = home[:, : items // 2].reshape(seq_devices, items, row_count)
    d_value = home[:, items // 2 : items].reshape(seq_devices, items, row_count)
    both = home[:, items].astype(jnp.float32)
    both = both[:, 0] + both[:, 1]
    d_filter = jnp.sum(both.reshape(group_count, seq_devices // group_count, tap_count), axis=1)
    return (d_key.reshape(channels, row_count), d_value.reshape(channels, row_count), d_filter)


def solution(mesh):
    fine = Mesh(mesh.devices.reshape(tuple(SPLIT.values())), tuple(SPLIT))
    placed = (P(CH, SEQ),) * 6 + (P(CH, None),)

    return jax.shard_map(
        local,
        mesh=fine,
        in_specs=placed,
        out_specs=(P(CH, SEQ), P(CH, SEQ), P(CH, None)),
        check_vma=False,
    )
```

```python
import math

import jax
import jax.numpy as jnp
import numpy as np
from jax import lax
from jax.experimental import pallas as pl
from jax.experimental.pallas import tpu as pltpu
from jax.sharding import Mesh, PartitionSpec as P


SEQ = ("z", "x", "yh")
CH = ("yl", "core")
SPLIT = {"z": 8, "x": 4, "yh": 2, "yl": 4, "core": 2}
PARTS = ("x",)
SHIFTS = (0, 2, -1, 1)
VMEM = pl.BlockSpec(memory_space=pltpu.VMEM)
INNER = 128
HALF = 64
LINES = 72


def swap(value, axes):
    return lax.all_to_all(value, axes, split_axis=0, concat_axis=0, tiled=True)


def flip(value, axis, bit):
    count = SPLIT[axis]
    return lax.ppermute(value, axis, [(i, i ^ bit) for i in range(count)])


def high_low(table):
    high = table.astype(jnp.bfloat16)
    low = (table - high.astype(np.float64)).astype(jnp.bfloat16)
    return high, low


def spectral_tables():
    total = 2 * HALF * INNER
    lines = np.arange(LINES)[:, None]
    kept = (lines <= HALF).astype(np.float64)
    weight = np.where((lines == 0) | (lines == HALF), 1.0, 2.0) * kept / total
    blocks = np.arange(HALF)[None, :]
    turn = 2.0 * math.pi * (lines * blocks % (2 * HALF)) / (2 * HALF)
    first = np.concatenate([np.cos(turn) * kept, -np.sin(turn) * kept])
    last = np.concatenate([np.cos(turn) * weight, -np.sin(turn) * weight]).T
    place = np.arange(INNER)
    twist = 2.0 * math.pi * (lines * place[None, :] % total) / total
    inner = 2.0 * math.pi * (place[:, None] * place[None, :] % INNER) / INNER
    cos_q, sin_q = np.cos(inner), np.sin(inner)
    middle = np.block([[cos_q, -sin_q], [sin_q, cos_q]])
    first_high, first_low = high_low(first)
    last_high, last_low = high_low(last)
    middle_high, middle_low = high_low(middle)
    return (
        np.concatenate([first_high, first_low], axis=1),
        np.concatenate([last_high, last_high, last_low], axis=1),
        middle_high,
        middle_low,
        np.cos(twist).astype(np.float32),
        np.sin(twist).astype(np.float32),
    )


def dot(first, second, first_dim=1, second_dim=0):
    return lax.dot_general(
        first,
        second,
        (((first_dim,), (second_dim,)), ((), ())),
        preferred_element_type=jnp.float32,
    )


def two_parts(value):
    high = value.astype(jnp.bfloat16)
    return high, (value - high.astype(jnp.float32)).astype(jnp.bfloat16)


def product(value, table_high, table_low, table_dim):
    high, low = two_parts(value)
    return (
        dot(high, table_high, 1, table_dim)
        + dot(high, table_low, 1, table_dim)
        + dot(low, table_high, 1, table_dim)
    )


def spectrum(rows_ref, items, first, middle_high, middle_low, cos_t, sin_t):
    series = jnp.concatenate(
        [rows_ref[pl.ds(c, HALF, stride=items), :] for c in range(items)], axis=1
    ).astype(jnp.bfloat16)
    lines = dot(first, jnp.concatenate([series, series], axis=0))
    turned = []
    for c in range(items):
        at = slice(c * INNER, (c + 1) * INNER)
        real, imag = lines[:LINES, at], lines[LINES:, at]
        turned.append(
            jnp.concatenate([real * cos_t + imag * sin_t, imag * cos_t - real * sin_t], axis=1)
        )
    return product(jnp.concatenate(turned, axis=0), middle_high, middle_low, 0)


def conv_kernel(
    scale,
    near,
    home_ref,
    taps_ref,
    back_taps_ref,
    first_ref,
    last_ref,
    high_ref,
    low_ref,
    cos_ref,
    sin_ref,
    out_ref,
    rows_ref,
    back_ref,
):
    count, inner = rows_ref.shape
    items = count // HALF
    parts = home_ref.shape[1] // items - 4
    shards = parts

    def two(place):
        both = home_ref[:, place * items : (place + 2) * items].astype(jnp.float32)
        return [half.reshape(count, inner) for half in (both[:, :items], both[:, items:])]

    filters, keys = two(shards)
    values, gates = two(shards + 2)
    first = first_ref[...]
    cos_t, sin_t = cos_ref[...], sin_ref[...]
    high, low = high_ref[...], low_ref[...]
    rows_ref[...] = filters
    filt = spectrum(rows_ref, items, first, high, low, cos_t, sin_t)
    filt_re, filt_im = filt[:, :inner], filt[:, inner:]
    values = values.astype(jnp.bfloat16)
    before = dot(values, back_taps_ref[:, :inner], 1, 1)
    filtered = dot(values, back_taps_ref[:, inner:], 1, 1)
    filtered += jnp.concatenate([jnp.zeros((items, inner), jnp.float32), before[:-items]], axis=0)
    for far in range(HALF // (parts * near)):
        for side in range(near):
            for shard in range(0, shards, 2):
                at = slice(shard * items, (shard + 2) * items)
                total = home_ref[far * parts * near + side, at].astype(jnp.float32)
                for p in range(1, parts):
                    total += home_ref[(far * parts + p) * near + side, at].astype(jnp.float32)
                for i in range(2):
                    block = (far * shards + shard + i) * near + side
                    at = slice(block * items, (block + 1) * items)
                    piece = (total[i * items : (i + 1) * items] * gates[at]).astype(jnp.bfloat16)
                    rows_ref[at] = piece.astype(jnp.float32)
    grad = spectrum(rows_ref, items, first, high, low, cos_t, sin_t)
    grad_re, grad_im = grad[:, :inner], grad[:, inner:]
    both = jnp.concatenate(
        [filt_re * grad_re + filt_im * grad_im, filt_re * grad_im - filt_im * grad_re], axis=1
    )
    both = product(both, high, low, 1)
    lines = []
    for c in range(items):
        at = slice(c * LINES, (c + 1) * LINES)
        real, imag = both[at, :inner], both[at, inner:]
        lines.append(
            jnp.concatenate([real * cos_t - imag * sin_t, imag * cos_t + real * sin_t], axis=0)
        )
    line_high, line_low = two_parts(jnp.concatenate(lines, axis=1))
    result = dot(last_ref[...], jnp.concatenate([line_high, line_low, line_high], axis=0))
    for c in range(items):
        back_ref[pl.ds(c, HALF, stride=items), :] = result[:, c * inner : (c + 1) * inner]
    d_w = back_ref[...].astype(jnp.bfloat16).astype(jnp.float32)
    d_key = d_w * filtered
    d_vf = (d_w * keys).astype(jnp.bfloat16).astype(jnp.float32)
    ahead = jnp.concatenate([d_vf[items:], jnp.zeros((items, inner), jnp.float32)], axis=0)
    pair = jnp.concatenate([d_vf, ahead], axis=1).astype(jnp.bfloat16)
    d_value = dot(pair, taps_ref[...], 1, 1)
    corr = dot(pair, values, 0, 0)
    corr = jnp.concatenate([corr[inner:], corr[:inner]], axis=1)
    row = lax.broadcasted_iota(jnp.int32, corr.shape, 0)
    shift = 1
    while shift < inner:
        moved = pltpu.roll(corr, 2 * inner - shift, 1)
        corr = jnp.where((row & shift) != 0, moved, corr)
        shift *= 2
    sums = jnp.sum(corr, axis=0, keepdims=True) * scale
    sums = pltpu.roll(jnp.broadcast_to(sums, (16, 2 * inner)), 2 * inner - 1, 1)[:, :inner]
    sum_high = sums.astype(jnp.bfloat16).astype(jnp.float32)
    line = lax.broadcasted_iota(jnp.int32, sums.shape, 0)
    sums = jnp.where(line == 0, sum_high, jnp.where(line == 1, sums - sum_high, 0.0))
    across = lax.broadcasted_iota(jnp.int32, (inner, inner), 0)
    across = across + lax.broadcasted_iota(jnp.int32, (inner, inner), 1)
    mirror = jnp.where(across == inner - 1, 1.0, 0.0).astype(jnp.bfloat16)
    sums = dot(sums.astype(jnp.bfloat16), mirror)[:items]
    both = [d_key.reshape(HALF, items, inner), d_value.reshape(HALF, items, inner)]
    out_ref[:, 0 : 2 * items, :] = jnp.concatenate(both, axis=1).astype(jnp.bfloat16)
    out_ref[:, 2 * items :, :] = jnp.broadcast_to(sums[None], (HALF, items, inner)).astype(
        jnp.bfloat16
    )


def project_kernel(mine_ref, other_ref, *rest):
    block_refs, own_refs, (out_ref, held_ref) = rest[:4], rest[4:-2], rest[-2:]
    shards, lines, _, rows = mine_ref.shape
    z, core, yh = lax.axis_index("z"), lax.axis_index("core"), lax.axis_index("yh")
    features = block_refs[0].shape[1]
    for shift, block_ref in zip(SHIFTS, block_refs):
        for e in range(4):
            source = ((z - shift) & 7) ^ (4 * (e // 2))
            if shift == 2:
                source = source ^ (4 * (z & 1))
            place = (source & 6) + ((source & 1) ^ core)
            at = pl.multiple_of((2 * place + (yh ^ (e % 2))) * features, features)
            held_ref[pl.ds(at, features), :] = block_ref[e]
    weight = held_ref[...].T
    dests = out_ref.shape[0]
    items = out_ref.shape[1] // (shards + len(own_refs))
    for i in range(0, len(own_refs), 2):
        both = [own_ref[...].astype(jnp.float32) for own_ref in own_refs[i : i + 2]]
        at = slice((shards + i) * items, (shards + i + 2) * items)
        out_ref[:, at] = jnp.concatenate(both, axis=1).astype(jnp.bfloat16)
    for s in range(0, shards, 2):
        columns = []
        for t in (s, s + 1):
            stack = []
            for y in range(lines):
                stack += [mine_ref[t, y], other_ref[t, y]]
            columns.append(jnp.concatenate(stack, axis=0))
        result = dot(weight, jnp.concatenate(columns, axis=1))
        both = [result[:, at : at + rows].reshape(dests, items, rows) for at in (0, rows)]
        at = slice(s * items, (s + 2) * items)
        out_ref[:, at] = jnp.concatenate(both, axis=1).astype(jnp.bfloat16)


def repeat_kernel(grad_ref, out_ref):
    for y in range(out_ref.shape[1]):
        out_ref[:, y] = grad_ref[...]


def local(queries, key_feat, value_feat, out_grad, out_weight, long_filter, short_filter):
    channels, row_count = out_grad.shape
    group_count, tap_count = short_filter.shape
    per_group = channels // group_count
    split = math.prod(SPLIT[a] for a in PARTS)
    seq_devices = SPLIT["z"] * SPLIT["x"] * SPLIT["yh"]
    items = channels // seq_devices
    depth = channels // split

    count_z = SPLIT["z"]
    weight = out_weight.T
    beside = flip(weight, "yh", 1)
    pair = jnp.stack([weight, beside])
    opposite = flip(pair, "z", 4)
    blocks = [jnp.concatenate([pair, opposite])]
    for k in SHIFTS[1:]:
        turn = [(-k if k == 2 and i % 2 else k) for i in range(count_z)]
        ring = [(i, (i + turn[i]) % count_z) for i in range(count_z)]
        blocks.append(lax.ppermute(blocks[0], "z", ring))

    grad = pl.pallas_call(
        repeat_kernel,
        out_shape=jax.ShapeDtypeStruct((split, SPLIT["yl"], depth, row_count), jnp.bfloat16),
        in_specs=[VMEM],
        out_specs=VMEM,
        compiler_params=pltpu.CompilerParams(vmem_limit_bytes=4 << 20),
        name="repeat",
    )(out_grad.reshape(split, depth, row_count))
    grad = swap(grad.reshape(split * SPLIT["yl"], depth, row_count), PARTS + ("yl",))
    other = flip(grad, "core", 1)
    form = (split, SPLIT["yl"], depth, row_count)

    pieces = [
        a.reshape(seq_devices, items, row_count)
        for a in (long_filter, key_feat, value_feat, queries)
    ]
    partial = pl.pallas_call(
        project_kernel,
        out_shape=jax.ShapeDtypeStruct((seq_devices, (split + 4) * items, row_count), jnp.bfloat16),
        in_specs=[VMEM] * 10,
        out_specs=VMEM,
        scratch_shapes=[pltpu.VMEM((8 * depth, channels), jnp.bfloat16)],
        cost_estimate=pl.CostEstimate(
            flops=2 * channels * 8 * depth * split * row_count, bytes_accessed=3 << 20, transcendentals=0
        ),
        compiler_params=pltpu.CompilerParams(vmem_limit_bytes=24 << 20),
        name="project",
    )(grad.reshape(form), other.reshape(form), *blocks, *pieces)
    partial = swap(partial, SEQ)
    near = seq_devices // (SPLIT["z"] * split)
    near = seq_devices // (SPLIT["z"] * split)

    place = lax.axis_index(SEQ) * items // per_group
    taps = lax.dynamic_slice_in_dim(short_filter, place, 1, 0)
    padded = jnp.pad(taps[0], (0, tap_count + 1))
    toeplitz = jnp.tile(padded, tap_count)[: 2 * tap_count * tap_count]
    toeplitz = toeplitz.reshape(tap_count, 2 * tap_count)
    first, last, high, low, cos_t, sin_t = spectral_tables()
    count = seq_devices * items
    scale = 1.0 / math.sqrt(row_count * seq_devices * per_group)

    def conv(*refs):
        conv_kernel(scale, near, *refs)

    home = pl.pallas_call(
        conv,
        out_shape=jax.ShapeDtypeStruct((seq_devices, 3 * items, row_count), jnp.bfloat16),
        in_specs=[VMEM] * 9,
        out_specs=VMEM,
        scratch_shapes=[pltpu.VMEM((count, row_count), jnp.float32)] * 2,
        cost_estimate=pl.CostEstimate(flops=1 << 31, bytes_accessed=4 << 20, transcendentals=0),
        compiler_params=pltpu.CompilerParams(vmem_limit_bytes=24 << 20),
        name="conv",
    )(partial, toeplitz, toeplitz[::-1, ::-1], first, last, high, low, cos_t, sin_t)
    home = home.reshape(seq_devices, 3 * items // 2, 2, row_count)[:, : items + 1]
    home = swap(home, SEQ)
    d_key = home[:, : items // 2].reshape(seq_devices, items, row_count)
    d_value = home[:, items // 2 : items].reshape(seq_devices, items, row_count)
    both = home[:, items].astype(jnp.float32)
    both = both[:, 0] + both[:, 1]
    d_filter = jnp.sum(both.reshape(group_count, seq_devices // group_count, tap_count), axis=1)
    return (d_key.reshape(channels, row_count), d_value.reshape(channels, row_count), d_filter)


def solution(mesh):
    fine = Mesh(mesh.devices.reshape(tuple(SPLIT.values())), tuple(SPLIT))
    placed = (P(CH, SEQ),) * 6 + (P(CH, None),)

    return jax.shard_map(
        local,
        mesh=fine,
        in_specs=placed,
        out_specs=(P(CH, SEQ), P(CH, SEQ), P(CH, None)),
        check_vma=False,
    )
```

```python
import math

import jax
import jax.numpy as jnp
import numpy as np
from jax import lax
from jax.experimental import pallas as pl
from jax.experimental.pallas import tpu as pltpu
from jax.sharding import Mesh, PartitionSpec as P


SEQ = ("z", "x", "yh")
CH = ("yl", "core")
SPLIT = {"z": 8, "x": 4, "yh": 2, "yl": 4, "core": 2}
PARTS = ("x",)
SHIFTS = (0, 2, -1, 1)
VMEM = pl.BlockSpec(memory_space=pltpu.VMEM)
INNER = 128
HALF = 64
LINES = 72


def swap(value, axes):
    return lax.all_to_all(value, axes, split_axis=0, concat_axis=0, tiled=True)


def flip(value, axis, bit):
    count = SPLIT[axis]
    return lax.ppermute(value, axis, [(i, i ^ bit) for i in range(count)])


def high_low(table):
    high = table.astype(jnp.bfloat16)
    low = (table - high.astype(np.float64)).astype(jnp.bfloat16)
    return high, low


def spectral_tables():
    total = 2 * HALF * INNER
    lines = np.arange(LINES)[:, None]
    kept = (lines <= HALF).astype(np.float64)
    weight = np.where((lines == 0) | (lines == HALF), 1.0, 2.0) * kept / total
    blocks = np.arange(HALF)[None, :]
    turn = 2.0 * math.pi * (lines * blocks % (2 * HALF)) / (2 * HALF)
    first = np.concatenate([np.cos(turn) * kept, -np.sin(turn) * kept])
    last = np.concatenate([np.cos(turn) * weight, -np.sin(turn) * weight]).T
    place = np.arange(INNER)
    twist = 2.0 * math.pi * (lines * place[None, :] % total) / total
    inner = 2.0 * math.pi * (place[:, None] * place[None, :] % INNER) / INNER
    cos_q, sin_q = np.cos(inner), np.sin(inner)
    middle = np.block([[cos_q, -sin_q], [sin_q, cos_q]])
    first_high, first_low = high_low(first)
    last_high, last_low = high_low(last)
    middle_high, middle_low = high_low(middle)
    return (
        np.concatenate([first_high, first_low], axis=1),
        np.concatenate([last_high, last_high, last_low], axis=1),
        middle_high,
        middle_low,
        np.cos(twist).astype(np.float32),
        np.sin(twist).astype(np.float32),
    )


def dot(first, second, first_dim=1, second_dim=0):
    return lax.dot_general(
        first,
        second,
        (((first_dim,), (second_dim,)), ((), ())),
        preferred_element_type=jnp.float32,
    )


def two_parts(value):
    high = value.astype(jnp.bfloat16)
    return high, (value - high.astype(jnp.float32)).astype(jnp.bfloat16)


def product(value, table_high, table_low, table_dim):
    high, low = two_parts(value)
    return (
        dot(high, table_high, 1, table_dim)
        + dot(high, table_low, 1, table_dim)
        + dot(low, table_high, 1, table_dim)
    )


def spectrum(rows_ref, items, first, middle_high, middle_low, cos_t, sin_t):
    series = jnp.concatenate(
        [rows_ref[pl.ds(c, HALF, stride=items), :] for c in range(items)], axis=1
    ).astype(jnp.bfloat16)
    lines = dot(first, jnp.concatenate([series, series], axis=0))
    turned = []
    for c in range(items):
        at = slice(c * INNER, (c + 1) * INNER)
        real, imag = lines[:LINES, at], lines[LINES:, at]
        turned.append(
            jnp.concatenate([real * cos_t + imag * sin_t, imag * cos_t - real * sin_t], axis=1)
        )
    return product(jnp.concatenate(turned, axis=0), middle_high, middle_low, 0)


def conv_kernel(
    scale,
    near,
    home_ref,
    taps_ref,
    back_taps_ref,
    first_ref,
    last_ref,
    high_ref,
    low_ref,
    cos_ref,
    sin_ref,
    out_ref,
    rows_ref,
    back_ref,
):
    count, inner = rows_ref.shape
    items = count // HALF
    parts = home_ref.shape[1] // items - 4
    shards = parts

    def two(place):
        both = home_ref[:, place * items : (place + 2) * items].astype(jnp.float32)
        return [half.reshape(count, inner) for half in (both[:, :items], both[:, items:])]

    filters, keys = two(shards)
    values, gates = two(shards + 2)
    first = first_ref[...]
    cos_t, sin_t = cos_ref[...], sin_ref[...]
    high, low = high_ref[...], low_ref[...]
    rows_ref[...] = filters
    filt = spectrum(rows_ref, items, first, high, low, cos_t, sin_t)
    filt_re, filt_im = filt[:, :inner], filt[:, inner:]
    values = values.astype(jnp.bfloat16)
    before = dot(values, back_taps_ref[:, :inner], 1, 1)
    filtered = dot(values, back_taps_ref[:, inner:], 1, 1)
    filtered += jnp.concatenate([jnp.zeros((items, inner), jnp.float32), before[:-items]], axis=0)
    for far in range(HALF // (parts * near)):
        for side in range(near):
            for shard in range(0, shards, 2):
                at = slice(shard * items, (shard + 2) * items)
                total = home_ref[far * parts * near + side, at].astype(jnp.float32)
                for p in range(1, parts):
                    total += home_ref[(far * parts + p) * near + side, at].astype(jnp.float32)
                for i in range(2):
                    block = (far * shards + shard + i) * near + side
                    at = slice(block * items, (block + 1) * items)
                    piece = (total[i * items : (i + 1) * items] * gates[at]).astype(jnp.bfloat16)
                    rows_ref[at] = piece.astype(jnp.float32)
    grad = spectrum(rows_ref, items, first, high, low, cos_t, sin_t)
    grad_re, grad_im = grad[:, :inner], grad[:, inner:]
    both = jnp.concatenate(
        [filt_re * grad_re + filt_im * grad_im, filt_re * grad_im - filt_im * grad_re], axis=1
    )
    both = product(both, high, low, 1)
    lines = []
    for c in range(items):
        at = slice(c * LINES, (c + 1) * LINES)
        real, imag = both[at, :inner], both[at, inner:]
        lines.append(
            jnp.concatenate([real * cos_t - imag * sin_t, imag * cos_t + real * sin_t], axis=0)
        )
    line_high, line_low = two_parts(jnp.concatenate(lines, axis=1))
    result = dot(last_ref[...], jnp.concatenate([line_high, line_low, line_high], axis=0))
    for c in range(items):
        back_ref[pl.ds(c, HALF, stride=items), :] = result[:, c * inner : (c + 1) * inner]
    d_w = back_ref[...].astype(jnp.bfloat16).astype(jnp.float32)
    d_key = d_w * filtered
    d_vf = (d_w * keys).astype(jnp.bfloat16).astype(jnp.float32)
    ahead = jnp.concatenate([d_vf[items:], jnp.zeros((items, inner), jnp.float32)], axis=0)
    pair = jnp.concatenate([d_vf, ahead], axis=1).astype(jnp.bfloat16)
    d_value = dot(pair, taps_ref[...], 1, 1)
    corr = dot(pair, values, 0, 0)
    corr = jnp.concatenate([corr[inner:], corr[:inner]], axis=1)
    row = lax.broadcasted_iota(jnp.int32, corr.shape, 0)
    shift = 1
    while shift < inner:
        moved = pltpu.roll(corr, 2 * inner - shift, 1)
        corr = jnp.where((row & shift) != 0, moved, corr)
        shift *= 2
    sums = jnp.sum(corr, axis=0, keepdims=True) * scale
    sums = pltpu.roll(jnp.broadcast_to(sums, (16, 2 * inner)), 2 * inner - 1, 1)[:, :inner]
    sum_high = sums.astype(jnp.bfloat16).astype(jnp.float32)
    line = lax.broadcasted_iota(jnp.int32, sums.shape, 0)
    sums = jnp.where(line == 0, sum_high, jnp.where(line == 1, sums - sum_high, 0.0))
    across = lax.broadcasted_iota(jnp.int32, (inner, inner), 0)
    across = across + lax.broadcasted_iota(jnp.int32, (inner, inner), 1)
    mirror = jnp.where(across == inner - 1, 1.0, 0.0).astype(jnp.bfloat16)
    sums = dot(sums.astype(jnp.bfloat16), mirror)[:items]
    both = [d_key.reshape(HALF, items, inner), d_value.reshape(HALF, items, inner)]
    out_ref[:, 0 : 2 * items, :] = jnp.concatenate(both, axis=1).astype(jnp.bfloat16)
    out_ref[:, 2 * items :, :] = jnp.broadcast_to(sums[None], (HALF, items, inner)).astype(
        jnp.bfloat16
    )


def project_kernel(mine_ref, other_ref, *rest):
    block_refs, own_refs, (out_ref, held_ref) = rest[:4], rest[4:-2], rest[-2:]
    shards, lines, _, rows = mine_ref.shape
    z, core, yh = lax.axis_index("z"), lax.axis_index("core"), lax.axis_index("yh")
    features = block_refs[0].shape[1]
    for shift, block_ref in zip(SHIFTS, block_refs):
        for e in range(4):
            source = ((z - shift) & 7) ^ (4 * (e % 2))
            if shift == 2:
                source = source ^ (4 * (z & 1))
            place = (source & 6) + ((source & 1) ^ core)
            at = pl.multiple_of((2 * place + (yh ^ (e // 2))) * features, features)
            held_ref[pl.ds(at, features), :] = block_ref[e]
    weight = held_ref[...].T
    dests = out_ref.shape[0]
    items = out_ref.shape[1] // (shards + len(own_refs))
    for i in range(0, len(own_refs), 2):
        both = [own_ref[...].astype(jnp.float32) for own_ref in own_refs[i : i + 2]]
        at = slice((shards + i) * items, (shards + i + 2) * items)
        out_ref[:, at] = jnp.concatenate(both, axis=1).astype(jnp.bfloat16)
    for s in range(0, shards, 2):
        columns = []
        for t in (s, s + 1):
            stack = []
            for y in range(lines):
                stack += [mine_ref[t, y], other_ref[t, y]]
            columns.append(jnp.concatenate(stack, axis=0))
        result = dot(weight, jnp.concatenate(columns, axis=1))
        both = [result[:, at : at + rows].reshape(dests, items, rows) for at in (0, rows)]
        at = slice(s * items, (s + 2) * items)
        out_ref[:, at] = jnp.concatenate(both, axis=1).astype(jnp.bfloat16)


def repeat_kernel(grad_ref, out_ref):
    for y in range(out_ref.shape[1]):
        out_ref[:, y] = grad_ref[...]


def local(queries, key_feat, value_feat, out_grad, out_weight, long_filter, short_filter):
    channels, row_count = out_grad.shape
    group_count, tap_count = short_filter.shape
    per_group = channels // group_count
    split = math.prod(SPLIT[a] for a in PARTS)
    seq_devices = SPLIT["z"] * SPLIT["x"] * SPLIT["yh"]
    items = channels // seq_devices
    depth = channels // split

    count_z = SPLIT["z"]
    weight = out_weight.T
    beside = flip(weight, "z", 4)
    pair = jnp.stack([weight, beside])
    opposite = flip(pair, "yh", 1)
    blocks = [jnp.concatenate([pair, opposite])]
    for k in SHIFTS[1:]:
        turn = [(-k if k == 2 and i % 2 else k) for i in range(count_z)]
        ring = [(i, (i + turn[i]) % count_z) for i in range(count_z)]
        blocks.append(lax.ppermute(blocks[0], "z", ring))

    grad = pl.pallas_call(
        repeat_kernel,
        out_shape=jax.ShapeDtypeStruct((split, SPLIT["yl"], depth, row_count), jnp.bfloat16),
        in_specs=[VMEM],
        out_specs=VMEM,
        compiler_params=pltpu.CompilerParams(vmem_limit_bytes=4 << 20),
        name="repeat",
    )(out_grad.reshape(split, depth, row_count))
    grad = swap(grad.reshape(split * SPLIT["yl"], depth, row_count), PARTS + ("yl",))
    other = flip(grad, "core", 1)
    form = (split, SPLIT["yl"], depth, row_count)

    pieces = [
        a.reshape(seq_devices, items, row_count)
        for a in (long_filter, key_feat, value_feat, queries)
    ]
    partial = pl.pallas_call(
        project_kernel,
        out_shape=jax.ShapeDtypeStruct((seq_devices, (split + 4) * items, row_count), jnp.bfloat16),
        in_specs=[VMEM] * 10,
        out_specs=VMEM,
        scratch_shapes=[pltpu.VMEM((8 * depth, channels), jnp.bfloat16)],
        cost_estimate=pl.CostEstimate(
            flops=2 * channels * 8 * depth * split * row_count, bytes_accessed=3 << 20, transcendentals=0
        ),
        compiler_params=pltpu.CompilerParams(vmem_limit_bytes=24 << 20),
        name="project",
    )(grad.reshape(form), other.reshape(form), *blocks, *pieces)
    partial = swap(partial, SEQ)
    near = seq_devices // (SPLIT["z"] * split)
    near = seq_devices // (SPLIT["z"] * split)

    place = lax.axis_index(SEQ) * items // per_group
    taps = lax.dynamic_slice_in_dim(short_filter, place, 1, 0)
    padded = jnp.pad(taps[0], (0, tap_count + 1))
    toeplitz = jnp.tile(padded, tap_count)[: 2 * tap_count * tap_count]
    toeplitz = toeplitz.reshape(tap_count, 2 * tap_count)
    back_taps = toeplitz[::-1, ::-1]
    first, last, high, low, cos_t, sin_t = spectral_tables()
    count = seq_devices * items
    scale = 1.0 / math.sqrt(row_count * seq_devices * per_group)

    def conv(*refs):
        conv_kernel(scale, near, *refs)

    home = pl.pallas_call(
        conv,
        out_shape=jax.ShapeDtypeStruct((seq_devices, 3 * items, row_count), jnp.bfloat16),
        in_specs=[VMEM] * 9,
        out_specs=VMEM,
        scratch_shapes=[pltpu.VMEM((count, row_count), jnp.float32)] * 2,
        cost_estimate=pl.CostEstimate(flops=1 << 31, bytes_accessed=4 << 20, transcendentals=0),
        compiler_params=pltpu.CompilerParams(vmem_limit_bytes=24 << 20),
        name="conv",
    )(partial, toeplitz, back_taps, first, last, high, low, cos_t, sin_t)
    home = home.reshape(seq_devices, 3 * items // 2, 2, row_count)[:, : items + 1]
    home = swap(home, SEQ)
    d_key = home[:, : items // 2].reshape(seq_devices, items, row_count)
    d_value = home[:, items // 2 : items].reshape(seq_devices, items, row_count)
    both = home[:, items].astype(jnp.float32)
    both = both[:, 0] + both[:, 1]
    d_filter = jnp.sum(both.reshape(group_count, seq_devices // group_count, tap_count), axis=1)
    return (d_key.reshape(channels, row_count), d_value.reshape(channels, row_count), d_filter)


def solution(mesh):
    fine = Mesh(mesh.devices.reshape(tuple(SPLIT.values())), tuple(SPLIT))
    placed = (P(CH, SEQ),) * 6 + (P(CH, None),)

    return jax.shard_map(
        local,
        mesh=fine,
        in_specs=placed,
        out_specs=(P(CH, SEQ), P(CH, SEQ), P(CH, None)),
        check_vma=False,
    )
```

```python
import math

import jax
import jax.numpy as jnp
import numpy as np
from jax import lax
from jax.experimental import pallas as pl
from jax.experimental.pallas import tpu as pltpu
from jax.sharding import Mesh, PartitionSpec as P


SEQ = ("z", "x", "yh")
CH = ("yl", "core")
SPLIT = {"z": 8, "x": 4, "yh": 2, "yl": 4, "core": 2}
PARTS = ("x",)
SHIFTS = (0, 2, -1, 1)
VMEM = pl.BlockSpec(memory_space=pltpu.VMEM)
INNER = 128
HALF = 64
LINES = 72


def swap(value, axes):
    return lax.all_to_all(value, axes, split_axis=0, concat_axis=0, tiled=True)


def flip(value, axis, bit):
    count = SPLIT[axis]
    return lax.ppermute(value, axis, [(i, i ^ bit) for i in range(count)])


def high_low(table):
    high = table.astype(jnp.bfloat16)
    low = (table - high.astype(np.float64)).astype(jnp.bfloat16)
    return high, low


def spectral_tables():
    total = 2 * HALF * INNER
    lines = np.arange(LINES)[:, None]
    kept = (lines <= HALF).astype(np.float64)
    weight = np.where((lines == 0) | (lines == HALF), 1.0, 2.0) * kept / total
    blocks = np.arange(HALF)[None, :]
    turn = 2.0 * math.pi * (lines * blocks % (2 * HALF)) / (2 * HALF)
    first = np.concatenate([np.cos(turn) * kept, -np.sin(turn) * kept])
    last = np.concatenate([np.cos(turn) * weight, -np.sin(turn) * weight]).T
    place = np.arange(INNER)
    twist = 2.0 * math.pi * (lines * place[None, :] % total) / total
    inner = 2.0 * math.pi * (place[:, None] * place[None, :] % INNER) / INNER
    cos_q, sin_q = np.cos(inner), np.sin(inner)
    middle = np.block([[cos_q, -sin_q], [sin_q, cos_q]])
    first_high, first_low = high_low(first)
    last_high, last_low = high_low(last)
    middle_high, middle_low = high_low(middle)
    return (
        np.concatenate([first_high, first_low], axis=1),
        np.concatenate([last_high, last_high, last_low], axis=1),
        middle_high,
        middle_low,
        np.cos(twist).astype(np.float32),
        np.sin(twist).astype(np.float32),
    )


def dot(first, second, first_dim=1, second_dim=0):
    return lax.dot_general(
        first,
        second,
        (((first_dim,), (second_dim,)), ((), ())),
        preferred_element_type=jnp.float32,
    )


def two_parts(value):
    high = value.astype(jnp.bfloat16)
    return high, (value - high.astype(jnp.float32)).astype(jnp.bfloat16)


def product(value, table_high, table_low, table_dim):
    high, low = two_parts(value)
    return (
        dot(high, table_high, 1, table_dim)
        + dot(high, table_low, 1, table_dim)
        + dot(low, table_high, 1, table_dim)
    )


def spectrum(rows_ref, items, first, middle_high, middle_low, cos_t, sin_t):
    series = jnp.concatenate(
        [rows_ref[pl.ds(c, HALF, stride=items), :] for c in range(items)], axis=1
    ).astype(jnp.bfloat16)
    lines = dot(first, jnp.concatenate([series, series], axis=0))
    turned = []
    for c in range(items):
        at = slice(c * INNER, (c + 1) * INNER)
        real, imag = lines[:LINES, at], lines[LINES:, at]
        turned.append(
            jnp.concatenate([real * cos_t + imag * sin_t, imag * cos_t - real * sin_t], axis=1)
        )
    return product(jnp.concatenate(turned, axis=0), middle_high, middle_low, 0)


def conv_kernel(
    scale,
    near,
    home_ref,
    taps_ref,
    back_taps_ref,
    first_ref,
    last_ref,
    high_ref,
    low_ref,
    cos_ref,
    sin_ref,
    out_ref,
    rows_ref,
    back_ref,
):
    count, inner = rows_ref.shape
    items = count // HALF
    parts = home_ref.shape[1] // items - 4
    shards = parts

    def two(place):
        both = home_ref[:, place * items : (place + 2) * items].astype(jnp.float32)
        return [half.reshape(count, inner) for half in (both[:, :items], both[:, items:])]

    filters, keys = two(shards)
    values, gates = two(shards + 2)
    first = first_ref[...]
    cos_t, sin_t = cos_ref[...], sin_ref[...]
    high, low = high_ref[...], low_ref[...]
    rows_ref[...] = filters
    filt = spectrum(rows_ref, items, first, high, low, cos_t, sin_t)
    filt_re, filt_im = filt[:, :inner], filt[:, inner:]
    values = values.astype(jnp.bfloat16)
    before = dot(values, back_taps_ref[:, :inner], 1, 1)
    filtered = dot(values, back_taps_ref[:, inner:], 1, 1)
    filtered += jnp.concatenate([jnp.zeros((items, inner), jnp.float32), before[:-items]], axis=0)
    for far in range(HALF // (parts * near)):
        for side in range(near):
            for shard in range(0, shards, 2):
                at = slice(shard * items, (shard + 2) * items)
                total = home_ref[far * parts * near + side, at].astype(jnp.float32)
                for p in range(1, parts):
                    total += home_ref[(far * parts + p) * near + side, at].astype(jnp.float32)
                for i in range(2):
                    block = (far * shards + shard + i) * near + side
                    at = slice(block * items, (block + 1) * items)
                    piece = (total[i * items : (i + 1) * items] * gates[at]).astype(jnp.bfloat16)
                    rows_ref[at] = piece.astype(jnp.float32)
    grad = spectrum(rows_ref, items, first, high, low, cos_t, sin_t)
    grad_re, grad_im = grad[:, :inner], grad[:, inner:]
    both = jnp.concatenate(
        [filt_re * grad_re + filt_im * grad_im, filt_re * grad_im - filt_im * grad_re], axis=1
    )
    both = product(both, high, low, 1)
    lines = []
    for c in range(items):
        at = slice(c * LINES, (c + 1) * LINES)
        real, imag = both[at, :inner], both[at, inner:]
        lines.append(
            jnp.concatenate([real * cos_t - imag * sin_t, imag * cos_t + real * sin_t], axis=0)
        )
    line_high, line_low = two_parts(jnp.concatenate(lines, axis=1))
    result = dot(last_ref[...], jnp.concatenate([line_high, line_low, line_high], axis=0))
    for c in range(items):
        back_ref[pl.ds(c, HALF, stride=items), :] = result[:, c * inner : (c + 1) * inner]
    d_w = back_ref[...].astype(jnp.bfloat16).astype(jnp.float32)
    d_key = d_w * filtered
    d_vf = (d_w * keys).astype(jnp.bfloat16).astype(jnp.float32)
    ahead = jnp.concatenate([d_vf[items:], jnp.zeros((items, inner), jnp.float32)], axis=0)
    pair = jnp.concatenate([d_vf, ahead], axis=1).astype(jnp.bfloat16)
    d_value = dot(pair, taps_ref[...], 1, 1)
    corr = dot(pair, values, 0, 0)
    corr = jnp.concatenate([corr[inner:], corr[:inner]], axis=1)
    row = lax.broadcasted_iota(jnp.int32, corr.shape, 0)
    shift = 1
    while shift < inner:
        moved = pltpu.roll(corr, 2 * inner - shift, 1)
        corr = jnp.where((row & shift) != 0, moved, corr)
        shift *= 2
    sums = jnp.sum(corr, axis=0, keepdims=True) * scale
    sums = pltpu.roll(jnp.broadcast_to(sums, (16, 2 * inner)), 2 * inner - 1, 1)[:, :inner]
    sum_high = sums.astype(jnp.bfloat16).astype(jnp.float32)
    line = lax.broadcasted_iota(jnp.int32, sums.shape, 0)
    sums = jnp.where(line == 0, sum_high, jnp.where(line == 1, sums - sum_high, 0.0))
    across = lax.broadcasted_iota(jnp.int32, (inner, inner), 0)
    across = across + lax.broadcasted_iota(jnp.int32, (inner, inner), 1)
    mirror = jnp.where(across == inner - 1, 1.0, 0.0).astype(jnp.bfloat16)
    sums = dot(sums.astype(jnp.bfloat16), mirror)[:items]
    both = [d_key.reshape(HALF, items, inner), d_value.reshape(HALF, items, inner)]
    out_ref[:, 0 : 2 * items, :] = jnp.concatenate(both, axis=1).astype(jnp.bfloat16)
    out_ref[:, 2 * items :, :] = jnp.broadcast_to(sums[None], (HALF, items, inner)).astype(
        jnp.bfloat16
    )


def project_kernel(mine_ref, other_ref, *rest):
    block_refs, own_refs, (out_ref, held_ref) = rest[:4], rest[4:-2], rest[-2:]
    shards, lines, _, rows = mine_ref.shape
    z, core, yh = lax.axis_index("z"), lax.axis_index("core"), lax.axis_index("yh")
    features = block_refs[0].shape[1]
    for shift, block_ref in zip(SHIFTS, block_refs):
        for e in range(4):
            source = ((z - shift) & 7) ^ (4 * (e % 2))
            if shift == 2:
                source = source ^ (4 * (z & 1))
            place = (source & 6) + ((source & 1) ^ core)
            at = pl.multiple_of((2 * place + (yh ^ (e // 2))) * features, features)
            held_ref[pl.ds(at, features), :] = block_ref[e]
    weight = held_ref[...].T
    dests = out_ref.shape[0]
    items = out_ref.shape[1] // (shards + len(own_refs))
    for i in range(0, len(own_refs), 2):
        both = [own_ref[...].astype(jnp.float32) for own_ref in own_refs[i : i + 2]]
        at = slice((shards + i) * items, (shards + i + 2) * items)
        out_ref[:, at] = jnp.concatenate(both, axis=1).astype(jnp.bfloat16)
    for s in range(0, shards, 2):
        columns = []
        for t in (s, s + 1):
            stack = []
            for y in range(lines):
                stack += [mine_ref[t, y], other_ref[t, y]]
            columns.append(jnp.concatenate(stack, axis=0))
        result = dot(weight, jnp.concatenate(columns, axis=1))
        both = [result[:, at : at + rows].reshape(dests, items, rows) for at in (0, rows)]
        at = slice(s * items, (s + 2) * items)
        out_ref[:, at] = jnp.concatenate(both, axis=1).astype(jnp.bfloat16)


def repeat_kernel(grad_ref, out_ref):
    for y in range(out_ref.shape[1]):
        out_ref[:, y] = grad_ref[...]


def unpack_kernel(home_ref, key_ref, value_ref, filter_ref):
    half = key_ref.shape[1]
    key_ref[...] = home_ref[:, :half]
    value_ref[...] = home_ref[:, half : 2 * half]
    both = home_ref[:, 2 * half].astype(jnp.float32).reshape(filter_ref.shape[0], -1, filter_ref.shape[1])
    filter_ref[...] = jnp.sum(both, axis=1)


def local(queries, key_feat, value_feat, out_grad, out_weight, long_filter, short_filter):
    channels, row_count = out_grad.shape
    group_count, tap_count = short_filter.shape
    per_group = channels // group_count
    split = math.prod(SPLIT[a] for a in PARTS)
    seq_devices = SPLIT["z"] * SPLIT["x"] * SPLIT["yh"]
    items = channels // seq_devices
    depth = channels // split

    count_z = SPLIT["z"]
    weight = out_weight.T
    beside = flip(weight, "z", 4)
    pair = jnp.stack([weight, beside])
    opposite = flip(pair, "yh", 1)
    blocks = [jnp.concatenate([pair, opposite])]
    for k in SHIFTS[1:]:
        turn = [(-k if k == 2 and i % 2 else k) for i in range(count_z)]
        ring = [(i, (i + turn[i]) % count_z) for i in range(count_z)]
        blocks.append(lax.ppermute(blocks[0], "z", ring))

    grad = pl.pallas_call(
        repeat_kernel,
        out_shape=jax.ShapeDtypeStruct((split, SPLIT["yl"], depth, row_count), jnp.bfloat16),
        in_specs=[VMEM],
        out_specs=VMEM,
        compiler_params=pltpu.CompilerParams(vmem_limit_bytes=4 << 20),
        name="repeat",
    )(out_grad.reshape(split, depth, row_count))
    grad = swap(grad.reshape(split * SPLIT["yl"], depth, row_count), PARTS + ("yl",))
    other = flip(grad, "core", 1)
    form = (split, SPLIT["yl"], depth, row_count)

    pieces = [
        a.reshape(seq_devices, items, row_count)
        for a in (long_filter, key_feat, value_feat, queries)
    ]
    partial = pl.pallas_call(
        project_kernel,
        out_shape=jax.ShapeDtypeStruct((seq_devices, (split + 4) * items, row_count), jnp.bfloat16),
        in_specs=[VMEM] * 10,
        out_specs=VMEM,
        scratch_shapes=[pltpu.VMEM((8 * depth, channels), jnp.bfloat16)],
        cost_estimate=pl.CostEstimate(
            flops=2 * channels * 8 * depth * split * row_count, bytes_accessed=3 << 20, transcendentals=0
        ),
        compiler_params=pltpu.CompilerParams(vmem_limit_bytes=24 << 20),
        name="project",
    )(grad.reshape(form), other.reshape(form), *blocks, *pieces)
    partial = swap(partial, SEQ)
    near = seq_devices // (SPLIT["z"] * split)
    near = seq_devices // (SPLIT["z"] * split)

    place = lax.axis_index(SEQ) * items // per_group
    taps = lax.dynamic_slice_in_dim(short_filter, place, 1, 0)
    padded = jnp.pad(taps[0], (0, tap_count + 1))
    toeplitz = jnp.tile(padded, tap_count)[: 2 * tap_count * tap_count]
    toeplitz = toeplitz.reshape(tap_count, 2 * tap_count)
    back_taps = toeplitz[::-1, ::-1]
    first, last, high, low, cos_t, sin_t = spectral_tables()
    count = seq_devices * items
    scale = 1.0 / math.sqrt(row_count * seq_devices * per_group)

    def conv(*refs):
        conv_kernel(scale, near, *refs)

    home = pl.pallas_call(
        conv,
        out_shape=jax.ShapeDtypeStruct((seq_devices, 3 * items, row_count), jnp.bfloat16),
        in_specs=[VMEM] * 9,
        out_specs=VMEM,
        scratch_shapes=[pltpu.VMEM((count, row_count), jnp.float32)] * 2,
        cost_estimate=pl.CostEstimate(flops=1 << 31, bytes_accessed=4 << 20, transcendentals=0),
        compiler_params=pltpu.CompilerParams(vmem_limit_bytes=24 << 20),
        name="conv",
    )(partial, toeplitz, back_taps, first, last, high, low, cos_t, sin_t)
    home = home.reshape(seq_devices, 3 * items // 2, 2, row_count)[:, : items + 1]
    home = swap(home, SEQ)
    pairs = (seq_devices, items // 2, 2, row_count)
    d_key, d_value, d_filter = pl.pallas_call(
        unpack_kernel,
        out_shape=(
            jax.ShapeDtypeStruct(pairs, jnp.bfloat16),
            jax.ShapeDtypeStruct(pairs, jnp.bfloat16),
            jax.ShapeDtypeStruct((group_count, tap_count), jnp.float32),
        ),
        in_specs=[VMEM],
        out_specs=(VMEM,) * 3,
        compiler_params=pltpu.CompilerParams(vmem_limit_bytes=4 << 20),
        name="unpack",
    )(home)
    return (d_key.reshape(channels, row_count), d_value.reshape(channels, row_count), d_filter)


def solution(mesh):
    fine = Mesh(mesh.devices.reshape(tuple(SPLIT.values())), tuple(SPLIT))
    placed = (P(CH, SEQ),) * 6 + (P(CH, None),)

    return jax.shard_map(
        local,
        mesh=fine,
        in_specs=placed,
        out_specs=(P(CH, SEQ), P(CH, SEQ), P(CH, None)),
        check_vma=False,
    )
```

```python
import math

import jax
import jax.numpy as jnp
import numpy as np
from jax import lax
from jax.experimental import pallas as pl
from jax.experimental.pallas import tpu as pltpu
from jax.sharding import Mesh, PartitionSpec as P


SEQ = ("z", "x", "yh")
CH = ("yl", "core")
SPLIT = {"z": 8, "x": 4, "yh": 2, "yl": 4, "core": 2}
PARTS = ("x",)
SHIFTS = (0, 2, -1, 1)
VMEM = pl.BlockSpec(memory_space=pltpu.VMEM)
INNER = 128
HALF = 64
LINES = 72


def swap(value, axes):
    return lax.all_to_all(value, axes, split_axis=0, concat_axis=0, tiled=True)


def flip(value, axis, bit):
    count = SPLIT[axis]
    return lax.ppermute(value, axis, [(i, i ^ bit) for i in range(count)])


def high_low(table):
    high = table.astype(jnp.bfloat16)
    low = (table - high.astype(np.float64)).astype(jnp.bfloat16)
    return high, low


def spectral_tables():
    total = 2 * HALF * INNER
    lines = np.arange(LINES)[:, None]
    kept = (lines <= HALF).astype(np.float64)
    weight = np.where((lines == 0) | (lines == HALF), 1.0, 2.0) * kept / total
    blocks = np.arange(HALF)[None, :]
    turn = 2.0 * math.pi * (lines * blocks % (2 * HALF)) / (2 * HALF)
    first = np.concatenate([np.cos(turn) * kept, -np.sin(turn) * kept])
    last = np.concatenate([np.cos(turn) * weight, -np.sin(turn) * weight]).T
    place = np.arange(INNER)
    twist = 2.0 * math.pi * (lines * place[None, :] % total) / total
    inner = 2.0 * math.pi * (place[:, None] * place[None, :] % INNER) / INNER
    cos_q, sin_q = np.cos(inner), np.sin(inner)
    middle = np.block([[cos_q, -sin_q], [sin_q, cos_q]])
    first_high, first_low = high_low(first)
    last_high, last_low = high_low(last)
    middle_high, middle_low = high_low(middle)
    return (
        np.concatenate([first_high, first_low], axis=1),
        np.concatenate([last_high, last_high, last_low], axis=1),
        middle_high,
        middle_low,
        np.cos(twist).astype(np.float32),
        np.sin(twist).astype(np.float32),
    )


def dot(first, second, first_dim=1, second_dim=0):
    return lax.dot_general(
        first,
        second,
        (((first_dim,), (second_dim,)), ((), ())),
        preferred_element_type=jnp.float32,
    )


def two_parts(value):
    high = value.astype(jnp.bfloat16)
    return high, (value - high.astype(jnp.float32)).astype(jnp.bfloat16)


def product(value, table_high, table_low, table_dim):
    high, low = two_parts(value)
    return (
        dot(high, table_high, 1, table_dim)
        + dot(high, table_low, 1, table_dim)
        + dot(low, table_high, 1, table_dim)
    )


def spectrum(rows_refs, items, first, middle_high, middle_low, cos_t, sin_t):
    series = jnp.concatenate(
        [ref[pl.ds(c, HALF, stride=items), :] for ref in rows_refs for c in range(items)], axis=1
    ).astype(jnp.bfloat16)
    lines = dot(first, jnp.concatenate([series, series], axis=0))
    turned = []
    for c in range(len(rows_refs) * items):
        at = slice(c * INNER, (c + 1) * INNER)
        real, imag = lines[:LINES, at], lines[LINES:, at]
        turned.append(
            jnp.concatenate([real * cos_t + imag * sin_t, imag * cos_t - real * sin_t], axis=1)
        )
    return product(jnp.concatenate(turned, axis=0), middle_high, middle_low, 0)


def conv_kernel(
    scale,
    near,
    home_ref,
    taps_ref,
    back_taps_ref,
    first_ref,
    last_ref,
    high_ref,
    low_ref,
    cos_ref,
    sin_ref,
    out_ref,
    rows_ref,
    back_ref,
):
    count, inner = rows_ref.shape
    items = count // HALF
    parts = home_ref.shape[1] // items - 4
    shards = parts

    def two(place):
        both = home_ref[:, place * items : (place + 2) * items].astype(jnp.float32)
        return [half.reshape(count, inner) for half in (both[:, :items], both[:, items:])]

    filters, keys = two(shards)
    values, gates = two(shards + 2)
    first = first_ref[...]
    cos_t, sin_t = cos_ref[...], sin_ref[...]
    high, low = high_ref[...], low_ref[...]
    back_ref[...] = filters
    values = values.astype(jnp.bfloat16)
    before = dot(values, back_taps_ref[:, :inner], 1, 1)
    filtered = dot(values, back_taps_ref[:, inner:], 1, 1)
    filtered += jnp.concatenate([jnp.zeros((items, inner), jnp.float32), before[:-items]], axis=0)
    for far in range(HALF // (parts * near)):
        for side in range(near):
            for shard in range(0, shards, 2):
                at = slice(shard * items, (shard + 2) * items)
                total = home_ref[far * parts * near + side, at].astype(jnp.float32)
                for p in range(1, parts):
                    total += home_ref[(far * parts + p) * near + side, at].astype(jnp.float32)
                for i in range(2):
                    block = (far * shards + shard + i) * near + side
                    at = slice(block * items, (block + 1) * items)
                    piece = (total[i * items : (i + 1) * items] * gates[at]).astype(jnp.bfloat16)
                    rows_ref[at] = piece.astype(jnp.float32)
    both = spectrum((back_ref, rows_ref), items, first, high, low, cos_t, sin_t)
    filt, grad = both[: items * LINES], both[items * LINES :]
    filt_re, filt_im = filt[:, :inner], filt[:, inner:]
    grad_re, grad_im = grad[:, :inner], grad[:, inner:]
    both = jnp.concatenate(
        [filt_re * grad_re + filt_im * grad_im, filt_re * grad_im - filt_im * grad_re], axis=1
    )
    both = product(both, high, low, 1)
    lines = []
    for c in range(items):
        at = slice(c * LINES, (c + 1) * LINES)
        real, imag = both[at, :inner], both[at, inner:]
        lines.append(
            jnp.concatenate([real * cos_t - imag * sin_t, imag * cos_t + real * sin_t], axis=0)
        )
    line_high, line_low = two_parts(jnp.concatenate(lines, axis=1))
    result = dot(last_ref[...], jnp.concatenate([line_high, line_low, line_high], axis=0))
    for c in range(items):
        back_ref[pl.ds(c, HALF, stride=items), :] = result[:, c * inner : (c + 1) * inner]
    d_w = back_ref[...].astype(jnp.bfloat16).astype(jnp.float32)
    d_key = d_w * filtered
    d_vf = (d_w * keys).astype(jnp.bfloat16).astype(jnp.float32)
    ahead = jnp.concatenate([d_vf[items:], jnp.zeros((items, inner), jnp.float32)], axis=0)
    pair = jnp.concatenate([d_vf, ahead], axis=1).astype(jnp.bfloat16)
    d_value = dot(pair, taps_ref[...], 1, 1)
    corr = dot(pair, values, 0, 0)
    corr = jnp.concatenate([corr[inner:], corr[:inner]], axis=1)
    row = lax.broadcasted_iota(jnp.int32, corr.shape, 0)
    shift = 1
    while shift < inner:
        moved = pltpu.roll(corr, 2 * inner - shift, 1)
        corr = jnp.where((row & shift) != 0, moved, corr)
        shift *= 2
    sums = jnp.sum(corr, axis=0, keepdims=True) * scale
    sums = pltpu.roll(jnp.broadcast_to(sums, (16, 2 * inner)), 2 * inner - 1, 1)[:, :inner]
    sum_high = sums.astype(jnp.bfloat16).astype(jnp.float32)
    line = lax.broadcasted_iota(jnp.int32, sums.shape, 0)
    sums = jnp.where(line == 0, sum_high, jnp.where(line == 1, sums - sum_high, 0.0))
    across = lax.broadcasted_iota(jnp.int32, (inner, inner), 0)
    across = across + lax.broadcasted_iota(jnp.int32, (inner, inner), 1)
    mirror = jnp.where(across == inner - 1, 1.0, 0.0).astype(jnp.bfloat16)
    sums = dot(sums.astype(jnp.bfloat16), mirror)[:items]
    both = [d_key.reshape(HALF, items, inner), d_value.reshape(HALF, items, inner)]
    out_ref[:, 0 : 2 * items, :] = jnp.concatenate(both, axis=1).astype(jnp.bfloat16)
    out_ref[:, 2 * items :, :] = jnp.broadcast_to(sums[None], (HALF, items, inner)).astype(
        jnp.bfloat16
    )


def project_kernel(mine_ref, other_ref, *rest):
    block_refs, own_refs, (out_ref, held_ref) = rest[:4], rest[4:-2], rest[-2:]
    shards, lines, _, rows = mine_ref.shape
    z, core, yh = lax.axis_index("z"), lax.axis_index("core"), lax.axis_index("yh")
    features = block_refs[0].shape[1]
    for shift, block_ref in zip(SHIFTS, block_refs):
        for e in range(4):
            source = ((z - shift) & 7) ^ (4 * (e % 2))
            if shift == 2:
                source = source ^ (4 * (z & 1))
            place = (source & 6) + ((source & 1) ^ core)
            at = pl.multiple_of((2 * place + (yh ^ (e // 2))) * features, features)
            held_ref[pl.ds(at, features), :] = block_ref[e]
    weight = held_ref[...].T
    dests = out_ref.shape[0]
    items = out_ref.shape[1] // (shards + len(own_refs))
    for i in range(0, len(own_refs), 2):
        both = [own_ref[...].astype(jnp.float32) for own_ref in own_refs[i : i + 2]]
        at = slice((shards + i) * items, (shards + i + 2) * items)
        out_ref[:, at] = jnp.concatenate(both, axis=1).astype(jnp.bfloat16)
    for s in range(0, shards, 2):
        columns = []
        for t in (s, s + 1):
            stack = []
            for y in range(lines):
                stack += [mine_ref[t, y], other_ref[t, y]]
            columns.append(jnp.concatenate(stack, axis=0))
        result = dot(weight, jnp.concatenate(columns, axis=1))
        both = [result[:, at : at + rows].reshape(dests, items, rows) for at in (0, rows)]
        at = slice(s * items, (s + 2) * items)
        out_ref[:, at] = jnp.concatenate(both, axis=1).astype(jnp.bfloat16)


def repeat_kernel(grad_ref, out_ref):
    for y in range(out_ref.shape[1]):
        out_ref[:, y] = grad_ref[...]


def unpack_kernel(home_ref, key_ref, value_ref, filter_ref):
    half = key_ref.shape[1]
    key_ref[...] = home_ref[:, :half]
    value_ref[...] = home_ref[:, half : 2 * half]
    both = home_ref[:, 2 * half].astype(jnp.float32).reshape(filter_ref.shape[0], -1, filter_ref.shape[1])
    filter_ref[...] = jnp.sum(both, axis=1)


def local(queries, key_feat, value_feat, out_grad, out_weight, long_filter, short_filter):
    channels, row_count = out_grad.shape
    group_count, tap_count = short_filter.shape
    per_group = channels // group_count
    split = math.prod(SPLIT[a] for a in PARTS)
    seq_devices = SPLIT["z"] * SPLIT["x"] * SPLIT["yh"]
    items = channels // seq_devices
    depth = channels // split

    count_z = SPLIT["z"]
    weight = out_weight.T
    beside = flip(weight, "z", 4)
    pair = jnp.stack([weight, beside])
    opposite = flip(pair, "yh", 1)
    blocks = [jnp.concatenate([pair, opposite])]
    for k in SHIFTS[1:]:
        turn = [(-k if k == 2 and i % 2 else k) for i in range(count_z)]
        ring = [(i, (i + turn[i]) % count_z) for i in range(count_z)]
        blocks.append(lax.ppermute(blocks[0], "z", ring))

    grad = pl.pallas_call(
        repeat_kernel,
        out_shape=jax.ShapeDtypeStruct((split, SPLIT["yl"], depth, row_count), jnp.bfloat16),
        in_specs=[VMEM],
        out_specs=VMEM,
        compiler_params=pltpu.CompilerParams(vmem_limit_bytes=4 << 20),
        name="repeat",
    )(out_grad.reshape(split, depth, row_count))
    grad = swap(grad.reshape(split * SPLIT["yl"], depth, row_count), PARTS + ("yl",))
    other = flip(grad, "core", 1)
    form = (split, SPLIT["yl"], depth, row_count)

    pieces = [
        a.reshape(seq_devices, items, row_count)
        for a in (long_filter, key_feat, value_feat, queries)
    ]
    partial = pl.pallas_call(
        project_kernel,
        out_shape=jax.ShapeDtypeStruct((seq_devices, (split + 4) * items, row_count), jnp.bfloat16),
        in_specs=[VMEM] * 10,
        out_specs=VMEM,
        scratch_shapes=[pltpu.VMEM((8 * depth, channels), jnp.bfloat16)],
        cost_estimate=pl.CostEstimate(
            flops=2 * channels * 8 * depth * split * row_count, bytes_accessed=3 << 20, transcendentals=0
        ),
        compiler_params=pltpu.CompilerParams(vmem_limit_bytes=24 << 20),
        name="project",
    )(grad.reshape(form), other.reshape(form), *blocks, *pieces)
    partial = swap(partial, SEQ)
    near = seq_devices // (SPLIT["z"] * split)
    near = seq_devices // (SPLIT["z"] * split)

    place = lax.axis_index(SEQ) * items // per_group
    taps = lax.dynamic_slice_in_dim(short_filter, place, 1, 0)
    padded = jnp.pad(taps[0], (0, tap_count + 1))
    toeplitz = jnp.tile(padded, tap_count)[: 2 * tap_count * tap_count]
    toeplitz = toeplitz.reshape(tap_count, 2 * tap_count)
    back_taps = toeplitz[::-1, ::-1]
    first, last, high, low, cos_t, sin_t = spectral_tables()
    count = seq_devices * items
    scale = 1.0 / math.sqrt(row_count * seq_devices * per_group)

    def conv(*refs):
        conv_kernel(scale, near, *refs)

    home = pl.pallas_call(
        conv,
        out_shape=jax.ShapeDtypeStruct((seq_devices, 3 * items, row_count), jnp.bfloat16),
        in_specs=[VMEM] * 9,
        out_specs=VMEM,
        scratch_shapes=[pltpu.VMEM((count, row_count), jnp.float32)] * 2,
        cost_estimate=pl.CostEstimate(flops=1 << 31, bytes_accessed=4 << 20, transcendentals=0),
        compiler_params=pltpu.CompilerParams(vmem_limit_bytes=24 << 20),
        name="conv",
    )(partial, toeplitz, back_taps, first, last, high, low, cos_t, sin_t)
    home = home.reshape(seq_devices, 3 * items // 2, 2, row_count)[:, : items + 1]
    home = swap(home, SEQ)
    pairs = (seq_devices, items // 2, 2, row_count)
    d_key, d_value, d_filter = pl.pallas_call(
        unpack_kernel,
        out_shape=(
            jax.ShapeDtypeStruct(pairs, jnp.bfloat16),
            jax.ShapeDtypeStruct(pairs, jnp.bfloat16),
            jax.ShapeDtypeStruct((group_count, tap_count), jnp.float32),
        ),
        in_specs=[VMEM],
        out_specs=(VMEM,) * 3,
        compiler_params=pltpu.CompilerParams(vmem_limit_bytes=4 << 20),
        name="unpack",
    )(home)
    return (d_key.reshape(channels, row_count), d_value.reshape(channels, row_count), d_filter)


def solution(mesh):
    fine = Mesh(mesh.devices.reshape(tuple(SPLIT.values())), tuple(SPLIT))
    placed = (P(CH, SEQ),) * 6 + (P(CH, None),)

    return jax.shard_map(
        local,
        mesh=fine,
        in_specs=placed,
        out_specs=(P(CH, SEQ), P(CH, SEQ), P(CH, None)),
        check_vma=False,
    )
```
